32 devices in a mesh: tok: 8 (over y, x, core), head: 4 (over z).
Axes of the slice: x: 2, y: 2, z: 4, core: 2. Of those that a mesh axis runs over, the one named last changes fastest.
Arguments:
- pre_tokens: bfloat16 [8192, 2048], P('tok'), may hold values from -6 to 6
- dec_tokens: bfloat16 [16, 2048], P('tok'), may hold values from -6 to 6
- attn_gain: float32 [2048], replicated, may hold values from 0.1 to 1.9
- mlp_gain: float32 [2048], replicated, may hold values from 0.1 to 1.9
- w_qkv: bfloat16 [3, 2048, 2048], P(None, 'head', 'tok'), may hold values from -0.125 to 0.125
- w_out: bfloat16 [2048, 2048], P('tok', 'head'), may hold values from -0.125 to 0.125
- w_gate_up: bfloat16 [2, 8192, 2048], P(None, 'head', 'tok'), may hold values from -0.125 to 0.125
- w_down: bfloat16 [2048, 8192], P('tok', 'head'), may hold values from -0.0625 to 0.0625
- pre_cache: bfloat16 [8, 2, 2048, 2048], P('tok', None, None, 'head'), may hold values from -60 to 60
- dec_cache: bfloat16 [16, 2, 4096, 2048], P('tok', None, None, 'head'), may hold values from -60 to 60
- pre_order: int32 [8], replicated, may hold values from 0 to 7, each once
- dec_order: int32 [16], replicated, may hold values from 0 to 15, each once
- pre_offsets: int32 [8], P('tok'), may hold values from 2 to 2048, as said below
- dec_lengths: int32 [16], P('tok'), may hold values from 2 to 4096, as said below
Outputs:
- pre_out: bfloat16 [8192, 2048], P('tok')
- dec_out: bfloat16 [16, 2048], P('tok')
The draws below stay inside these ranges and needn't reach their ends.
Inputs may be any that keep to these rules, and one draw needn't show every extreme that they name: `pre_order`: the prefill request at position k is handled with the caches of position k, which lie on index k of tok. `dec_order`: positions k of one index of tok are those with k // 2 equal to it. `pre_offsets`: some position reaches 2048. `dec_lengths`: some position reaches 4096.
All inputs are finite; a program needn't handle non-finite values.
Results may differ from the reference program's by a relative error of at most 0.013.
Values may be sent and summed in bfloat16 or wider, within the bound.
A program may use at most 192 MiB of HBM per device.

```python
import jax
import jax.numpy as jnp
from jax import lax

D = 2048
HEADS = 32
HD = 64
FF = 8192
SPAN = 1024
PREFIX = 2048
CACHE = 4096
PF = 8
DEC = 16
N_TOK = 8


def cache_draw(key, count, length):
    first_key = jax.random.fold_in(jax.random.fold_in(key, 7), 0)
    shape = (count, 2, length, HEADS * HD)
    return jnp.clip(jax.random.normal(first_key, shape, jnp.float32), -6.0, 6.0)


def draw_pre_cache(key, part):
    return cache_draw(key, PF, PREFIX).astype(jnp.bfloat16)


def draw_dec_cache(key, part):
    return cache_draw(key, DEC, CACHE).astype(jnp.bfloat16)


def bounded_counts(key, count, largest):
    first_key, second_key = jax.random.split(jax.random.fold_in(key, 11))
    values = jax.random.randint(first_key, (count,), 2, largest + 1)
    chosen = jax.random.randint(second_key, (), 0, count)
    return jnp.where(jnp.arange(count) == chosen, largest, values).astype(jnp.int32)


def draw_pre_offsets(key, part):
    return bounded_counts(key, PF, PREFIX)


def draw_dec_lengths(key, part):
    return bounded_counts(key, DEC, CACHE)


def level_of(stream_key, extent, cuts, smallest, top_value):
    loudness, own = 1.0, jax.random.fold_in(stream_key, 6)
    for axis_at, shards_of in cuts:
        heights = jnp.exp(jax.random.uniform(jax.random.fold_in(own, axis_at), (shards_of,), jnp.float32, smallest / len(cuts), top_value / len(cuts)))
        loudness = loudness * jnp.repeat(heights, extent[axis_at] // shards_of).reshape([-1 if axis == axis_at else 1 for axis in range(len(extent))])
    return loudness


def centred(own_key, shape, scale, bound, cuts=(), held_as=jnp.bfloat16):
    result = scale * jax.random.normal(own_key, shape, jnp.float32)
    if cuts:
        result = result * level_of(own_key, shape, cuts, -0.22, 0.18)
    return jnp.clip(result, -bound, bound).astype(held_as)


def setup_inputs(seed: int = 0) -> dict:
    keys = jax.random.split(jax.random.key(seed), 15)
    return {
        "pre_tokens": centred(keys[0], (PF * SPAN, D), 1.0, 6.0, ((0, 8),)),
        "dec_tokens": centred(keys[1], (DEC, D), 1.0, 6.0, ((0, 8),)),
        "attn_gain": jnp.clip(1.0 + 0.18 * jax.random.normal(keys[2], (D,), jnp.float32), 0.1, 1.9),
        "mlp_gain": jnp.clip(1.0 + 0.18 * jax.random.normal(keys[3], (D,), jnp.float32), 0.1, 1.9),
        "w_qkv": centred(keys[4], (3, HEADS * HD, D), D ** -0.5, 0.125, ((1, 4), (2, 8))),
        "w_out": centred(keys[5], (D, HEADS * HD), (HEADS * HD) ** -0.5, 0.125, ((0, 8), (1, 4))),
        "w_gate_up": centred(keys[6], (2, FF, D), D ** -0.5, 0.125, ((1, 4), (2, 8))),
        "w_down": centred(keys[7], (D, FF), FF ** -0.5, 0.0625, ((0, 8), (1, 4))),
        "pre_cache": draw_pre_cache(jax.random.fold_in(keys[14], 71), 0),
        "dec_cache": draw_dec_cache(jax.random.fold_in(keys[14], 71), 0),
        "pre_order": jax.random.permutation(keys[10], PF).astype(jnp.int32),
        "dec_order": jax.random.permutation(keys[11], DEC).astype(jnp.int32),
        "pre_offsets": draw_pre_offsets(jax.random.fold_in(keys[14], 71), 0),
        "dec_lengths": draw_dec_lengths(jax.random.fold_in(keys[14], 71), 0),
    }


rope_base = 130000.0
norm_eps = 1e-05

def rotate(values, positions):
    width = values.shape[-1]
    half = width // 2
    freqs = rope_base ** (-(jnp.arange(half, dtype=jnp.float32) * 2.0 / width))
    angles = positions.astype(jnp.float32)[:, None] * freqs[None, :]
    cosine = jnp.cos(angles)[:, None, :]
    sine = jnp.sin(angles)[:, None, :]
    first = values[..., :half]
    second = values[..., half:]
    return jnp.concatenate([first * cosine - second * sine, second * cosine + first * sine], axis=-1)

def rms_norm(rows, gain):
    rows = rows.astype(jnp.float32)
    factor = lax.rsqrt(lax.optimization_barrier(jnp.mean(rows * rows, axis=-1, keepdims=True)) + norm_eps)
    return (rows * factor * gain).astype(jnp.bfloat16)

def attend(query, keys_new, values_new, cache, limit, positions, self_mask):
    rows_q = query.shape[0]
    heads = query.shape[1]
    size = query.shape[2]
    q_rot = rotate(query.astype(jnp.float32), positions).astype(jnp.bfloat16)
    k_rot = rotate(keys_new.astype(jnp.float32), positions).astype(jnp.bfloat16)
    length = cache.shape[1]
    cached_keys = cache[0].reshape(length, heads, size)
    cached_values = cache[1].reshape(length, heads, size)
    all_keys = jnp.concatenate([cached_keys, k_rot], axis=0)
    all_values = jnp.concatenate([cached_values, values_new], axis=0)
    scores = jnp.einsum('qhd,khd->hqk', q_rot.astype(jnp.float32), all_keys.astype(jnp.float32)) / jnp.sqrt(jnp.float32(size))
    cache_live = jnp.broadcast_to(jnp.arange(length, dtype=jnp.int32)[None, :] < limit, (rows_q, length))
    valid = jnp.concatenate([cache_live, self_mask], axis=1)
    scores = jnp.where(valid[None], scores, -jnp.inf)
    top = lax.optimization_barrier(jnp.max(scores, axis=-1, keepdims=True))
    weights = jnp.exp(scores - top)
    total = lax.optimization_barrier(jnp.sum(weights, axis=-1))
    mixed = jnp.einsum('hqk,khd->qhd', weights.astype(jnp.bfloat16).astype(jnp.float32), all_values.astype(jnp.float32))
    mixed = mixed / jnp.transpose(total)[:, :, None]
    return mixed.astype(jnp.bfloat16).reshape(rows_q, heads * size)

def inverse_of(order, count):
    return jnp.zeros((count,), jnp.int32).at[order].set(jnp.arange(count, dtype=jnp.int32))

def reference(pre_tokens, dec_tokens, attn_gain, mlp_gain, w_qkv, w_out, w_gate_up, w_down, pre_cache, dec_cache, pre_order, dec_order, pre_offsets, dec_lengths):
    piece_len = SPAN // N_TOK
    width = HEADS * HD
    rows = jnp.concatenate([pre_tokens, dec_tokens], axis=0)
    normed = rms_norm(rows, attn_gain)
    projected = jnp.dot(normed, w_qkv.reshape(3 * width, D).T, preferred_element_type=jnp.float32).astype(jnp.bfloat16)
    projected = projected.reshape(-1, 3, HEADS, HD)
    pre_part = projected[:PF * SPAN].reshape(N_TOK, PF, piece_len, 3, HEADS, HD)
    pre_part = jnp.transpose(pre_part, (1, 0, 2, 3, 4, 5)).reshape(PF, SPAN, 3, HEADS, HD)
    by_position = pre_part[pre_order]
    causal = jnp.arange(SPAN, dtype=jnp.int32)[None, :] <= jnp.arange(SPAN, dtype=jnp.int32)[:, None]

    def prefill_one(item):
        block, cache, offset = item
        positions = offset + jnp.arange(SPAN, dtype=jnp.int32)
        return attend(block[:, 0], block[:, 1], block[:, 2], cache, offset, positions, causal)
    pre_att = lax.map(prefill_one, (by_position, pre_cache, pre_offsets))
    pre_att = pre_att[inverse_of(pre_order, PF)]
    pre_att = jnp.transpose(pre_att.reshape(PF, N_TOK, piece_len, width), (1, 0, 2, 3)).reshape(PF * SPAN, width)
    dec_part = projected[PF * SPAN:][dec_order]
    self_only = jnp.ones((1, 1), jnp.bool_)

    def decode_one(item):
        block, cache, length = item
        positions = jnp.reshape(length, (1,))
        return attend(block[None, 0], block[None, 1], block[None, 2], cache, length, positions, self_only)
    dec_att = lax.map(decode_one, (dec_part, dec_cache, dec_lengths)).reshape(DEC, width)
    dec_att = dec_att[inverse_of(dec_order, DEC)]
    attended = jnp.concatenate([pre_att, dec_att], axis=0)
    resid = rows.astype(jnp.float32) + jnp.dot(attended, w_out.T, preferred_element_type=jnp.float32)
    mlp_in = rms_norm(resid, mlp_gain)
    gate_up = jnp.dot(mlp_in, w_gate_up.reshape(2 * FF, D).T, preferred_element_type=jnp.float32)
    hidden = (jax.nn.silu(gate_up[:, :FF]) * gate_up[:, FF:]).astype(jnp.bfloat16)
    final = (resid + jnp.dot(hidden, w_down.T, preferred_element_type=jnp.float32)).astype(jnp.bfloat16)
    return (final[:PF * SPAN], final[PF * SPAN:])
```

```python
import jax
import jax.numpy as jnp
from jax import lax
from jax.experimental import pallas as pl
from jax.experimental.pallas import tpu as pltpu
from jax.sharding import PartitionSpec as P

HD = 64
Q_ROWS = 512
K_ROWS = 512
DEC_ROWS = 1024


rope_base = 130000.0
norm_eps = 1e-05
masked_score = -1e30


def rotate(values, positions):
    width = values.shape[-1]
    half = width // 2
    freqs = rope_base ** (-(jnp.arange(half, dtype=jnp.float32) * 2.0 / width))
    angles = positions.astype(jnp.float32)[:, None] * freqs[None, :]
    cosine = jnp.cos(angles)[:, None, :]
    sine = jnp.sin(angles)[:, None, :]
    first = values[..., :half]
    second = values[..., half:]
    return jnp.concatenate(
        [first * cosine - second * sine, second * cosine + first * sine], axis=-1
    )


def rms_norm(rows, gain):
    rows = rows.astype(jnp.float32)
    factor = lax.rsqrt(jnp.mean(rows * rows, axis=-1, keepdims=True) + norm_eps)
    return (rows * factor * gain).astype(jnp.bfloat16)


def fold_rows(inputs, weights):
    return jnp.einsum("td,kcd->ktc", inputs, weights, preferred_element_type=jnp.float32)


def map_rows(inputs, weights):
    return jnp.einsum("tc,dc->td", inputs, weights, preferred_element_type=jnp.float32)


def whole(weights, axis):
    return lax.all_gather(weights, "tok", axis=axis, tiled=True)


def over_heads(partial_value):
    return lax.psum(partial_value.astype(jnp.bfloat16), "head").astype(jnp.float32)


def rope_tables(positions, width):
    half = HD // 2
    freqs = rope_base ** (-(jnp.arange(half, dtype=jnp.float32) * 2.0 / HD))
    angles = positions.astype(jnp.float32)[:, None] * freqs[None, :]
    cosine = jnp.cos(angles)
    sine = jnp.sin(angles)
    copies = width // HD
    return (
        jnp.tile(jnp.concatenate([cosine, cosine], axis=1), (1, copies)),
        jnp.tile(jnp.concatenate([-sine, sine], axis=1), (1, copies)),
    )


def swap_halves(values):
    half = HD // 2
    width = values.shape[-1]
    lane = lax.broadcasted_iota(jnp.int32, values.shape, values.ndim - 1)
    axis = values.ndim - 1
    return jnp.where(
        lane % HD < half,
        pltpu.roll(values, width - half, axis),
        pltpu.roll(values, half, axis),
    )


def prefill_kernel(
    limit_ref, q_ref, k_ref, v_ref, cos_ref, sin_ref, cache_ref, out_ref, q_rot, k_rot, v_ext, c_ext
):
    span = q_ref.shape[1]
    length = cache_ref.shape[2]
    pair = q_ref.shape[2]
    limit = limit_ref[0]
    cosine = cos_ref[...]
    sine = sin_ref[...]
    lane = lax.broadcasted_iota(jnp.int32, (1, pair), 1)
    halves = (lane < HD, lane >= HD)

    key = k_ref[0].astype(jnp.float32)
    k_rot[...] = (key * cosine + swap_halves(key) * sine).astype(jnp.bfloat16)
    query = q_ref[0].astype(jnp.float32)
    query = (query * cosine + swap_halves(query) * sine).astype(jnp.bfloat16)
    query = query * jnp.bfloat16(HD**-0.5)
    one = jnp.ones((), jnp.bfloat16)
    zero = jnp.zeros((), jnp.bfloat16)
    for side in range(2):
        q_rot[side] = jnp.where(halves[side], query, zero)
        v_ext[side] = jnp.where(halves[side], v_ref[0], one)
        c_ext[side] = jnp.where(halves[side], cache_ref[0, 1], one)

    def score(rows, keys):
        return lax.dot_general(
            rows, keys, (((1,), (1,)), ((), ())), preferred_element_type=jnp.float32
        )

    def fold(state, scores, values):
        top, mixed = state
        new_top = jnp.maximum(top, jnp.max(scores, axis=-1, keepdims=True))
        weights = jnp.exp(scores - new_top).astype(jnp.bfloat16)
        factor = jnp.exp(top - new_top)
        return new_top, mixed * factor + jnp.dot(
            weights, values, preferred_element_type=jnp.float32
        )

    for block in range(span // Q_ROWS):
        start = block * Q_ROWS
        rows = [q_rot[side, start : start + Q_ROWS, :] for side in range(2)]
        keys = k_rot[start : start + Q_ROWS, :]
        shape = (Q_ROWS, Q_ROWS)
        seen = lax.broadcasted_iota(jnp.int32, shape, 1) <= lax.broadcasted_iota(
            jnp.int32, shape, 0
        )
        states = []
        for side in range(2):
            scores = jnp.where(seen, score(rows[side], keys), masked_score)
            top = jnp.max(scores, axis=-1, keepdims=True)
            weights = jnp.exp(scores - top).astype(jnp.bfloat16)
            mixed = jnp.dot(
                weights,
                v_ext[side, start : start + Q_ROWS, :],
                preferred_element_type=jnp.float32,
            )
            states.append((top, mixed))
        for earlier in range(block):
            begin = earlier * Q_ROWS
            keys = k_rot[begin : begin + Q_ROWS, :]
            for side in range(2):
                states[side] = fold(
                    states[side],
                    score(rows[side], keys),
                    v_ext[side, begin : begin + Q_ROWS, :],
                )

        def cached(index, state, masked):
            begin = pl.multiple_of(index * K_ROWS, K_ROWS)
            keys_now = cache_ref[0, 0, pl.ds(begin, K_ROWS), :]
            result = []
            for side in range(2):
                scores = score(rows[side], keys_now)
                if masked:
                    spot = begin + lax.broadcasted_iota(jnp.int32, (1, K_ROWS), 1)
                    scores = jnp.where(spot < limit, scores, masked_score)
                result.append(
                    fold(state[side], scores, c_ext[side, pl.ds(begin, K_ROWS), :])
                )
            return tuple(result)

        full = limit // K_ROWS
        every = (limit + K_ROWS - 1) // K_ROWS
        states = lax.fori_loop(0, full, lambda i, s: cached(i, s, False), tuple(states))
        states = lax.fori_loop(full, every, lambda i, s: cached(i, s, True), states)
        parts = []
        for side in range(2):
            mixed = states[side][1]
            total = pltpu.roll(mixed, HD, 1)
            parts.append(mixed / total)
        out_ref[start : start + Q_ROWS, :] = jnp.where(halves[0], parts[0], parts[1]).astype(
            jnp.bfloat16
        )


def prefill_attend(qkv, offset, cache):
    _, span, width = qkv.shape
    length = cache.shape[2]
    pair = 2 * HD
    cosine, sine = rope_tables(offset + jnp.arange(span, dtype=jnp.int32), pair)
    part = lambda which: pl.BlockSpec((1, span, pair), lambda p, limit: (which, 0, p))
    table = pl.BlockSpec((span, pair), lambda p, limit: (0, 0))
    return pl.pallas_call(
        prefill_kernel,
        out_shape=jax.ShapeDtypeStruct((span, width), jnp.bfloat16),
        grid_spec=pltpu.PrefetchScalarGridSpec(
            num_scalar_prefetch=1,
            grid=(width // pair,),
            in_specs=[
                part(0),
                part(1),
                part(2),
                table,
                table,
                pl.BlockSpec((1, 2, length, pair), lambda p, limit: (0, 0, 0, p)),
            ],
            out_specs=pl.BlockSpec((span, pair), lambda p, limit: (0, p)),
            scratch_shapes=[
                pltpu.VMEM((2, span, pair), jnp.bfloat16),
                pltpu.VMEM((span, pair), jnp.bfloat16),
                pltpu.VMEM((2, span, pair), jnp.bfloat16),
                pltpu.VMEM((2, length, pair), jnp.bfloat16),
            ],
        ),
        compiler_params=pltpu.CompilerParams(vmem_limit_bytes=40 * 1024 * 1024),
        cost_estimate=pl.CostEstimate(
            flops=16 * span * 3 * span * width,
            bytes_accessed=4 * length * width + 8 * span * width,
            transcendentals=span * 3 * span * width // HD,
        ),
        name="prefill_attend",
    )(offset[None], qkv, qkv, qkv, cosine, sine, cache)


def decode_kernel(limits_ref, q_ref, k_ref, v_ref, cache_ref, out_ref, top_ref, total_ref, mixed_ref):
    request = pl.program_id(0)
    index = pl.program_id(1)
    limit = limits_ref[request]
    heads, width = q_ref.shape[1:]
    block = cache_ref.shape[2]

    @pl.when(index == 0)
    def _():
        own = q_ref[0].astype(jnp.float32) * k_ref[0].astype(jnp.float32)
        top_ref[...] = jnp.sum(own, axis=-1, keepdims=True)
        total_ref[...] = jnp.ones_like(total_ref)
        mixed_ref[...] = jnp.broadcast_to(v_ref[0].astype(jnp.float32), (heads, width))

    @pl.when(index * block < limit)
    def _():
        scores = lax.dot_general(
            q_ref[0],
            cache_ref[0, 0],
            (((1,), (1,)), ((), ())),
            preferred_element_type=jnp.float32,
        )
        spot = index * block + lax.broadcasted_iota(jnp.int32, (1, block), 1)
        scores = jnp.where(spot < limit, scores, masked_score)
        top = top_ref[...]
        new_top = jnp.maximum(top, jnp.max(scores, axis=-1, keepdims=True))
        weights = jnp.exp(scores - new_top)
        factor = jnp.exp(top - new_top)
        top_ref[...] = new_top
        total_ref[...] = total_ref[...] * factor + jnp.sum(weights, axis=-1, keepdims=True)
        mixed_ref[...] = mixed_ref[...] * factor + jnp.dot(
            weights.astype(jnp.bfloat16), cache_ref[0, 1], preferred_element_type=jnp.float32
        )

    @pl.when(index == pl.num_programs(1) - 1)
    def _():
        shape = (heads, width)
        mine = lax.broadcasted_iota(jnp.int32, shape, 1) // HD == lax.broadcasted_iota(
            jnp.int32, shape, 0
        )
        value = jnp.where(mine, mixed_ref[...] / total_ref[...], 0.0)
        out_ref[0] = jnp.sum(value, axis=0, keepdims=True).astype(jnp.bfloat16)


def decode_attend(qkv, lengths, cache):
    _, count, width = qkv.shape
    heads = width // HD
    block = min(DEC_ROWS, cache.shape[2])
    split = qkv.reshape(3, count, heads, HD)
    q_rot = rotate(split[0].astype(jnp.float32), lengths).astype(jnp.bfloat16)
    k_rot = rotate(split[1].astype(jnp.float32), lengths).astype(jnp.bfloat16)
    q_rot = q_rot * jnp.bfloat16(HD**-0.5)
    spread = jnp.where(
        jnp.eye(heads, dtype=jnp.bool_)[None, :, :, None], q_rot[:, None], jnp.bfloat16(0)
    ).reshape(count, heads, width)

    def cache_at(request, index, limits):
        last = (limits[request] - 1) // block
        return (request, 0, jnp.minimum(index, last), 0)

    row = pl.BlockSpec((1, 1, width), lambda request, index, limits: (request, 0, 0))
    return pl.pallas_call(
        decode_kernel,
        out_shape=jax.ShapeDtypeStruct((count, 1, width), jnp.bfloat16),
        grid_spec=pltpu.PrefetchScalarGridSpec(
            num_scalar_prefetch=1,
            grid=(count, cache.shape[2] // block),
            in_specs=[
                pl.BlockSpec((1, heads, width), lambda request, index, limits: (request, 0, 0)),
                row,
                row,
                pl.BlockSpec((1, 2, block, width), cache_at),
            ],
            out_specs=row,
            scratch_shapes=[
                pltpu.VMEM((heads, 1), jnp.float32),
                pltpu.VMEM((heads, 1), jnp.float32),
                pltpu.VMEM((heads, width), jnp.float32),
            ],
        ),
        compiler_params=pltpu.CompilerParams(vmem_limit_bytes=32 * 1024 * 1024),
        cost_estimate=pl.CostEstimate(
            flops=4 * count * heads * cache.shape[2] * width,
            bytes_accessed=4 * count * cache.shape[2] * width,
            transcendentals=count * cache.shape[2] * heads,
        ),
        name="decode_attend",
    )(lengths, spread, k_rot.reshape(count, 1, width), qkv[2].reshape(count, 1, width), cache)[:, 0]


def on_device(
    pre_tokens,
    dec_tokens,
    attn_gain,
    mlp_gain,
    w_qkv,
    w_out,
    w_gate_up,
    w_down,
    pre_cache,
    dec_cache,
    pre_order,
    dec_order,
    pre_offsets,
    dec_lengths,
):
    tok_count = lax.axis_size("tok")
    tok_index = lax.axis_index("tok")
    span_rows = pre_tokens.shape[0]
    piece_len = span_rows // tok_count
    dec_local = dec_tokens.shape[0]
    dec_total = dec_order.shape[0]
    group_width = w_qkv.shape[1]
    rows = jnp.concatenate([pre_tokens, dec_tokens], axis=0)
    normed = rms_norm(rows, attn_gain)
    projected = fold_rows(normed, whole(w_qkv, 2)).astype(jnp.bfloat16)
    pre_part = projected[:, :span_rows].reshape(3, tok_count, piece_len, group_width)
    pre_send = jnp.take(pre_part, pre_order, axis=1)
    dec_part = projected[:, span_rows:]
    dec_send = jnp.broadcast_to(dec_part[:, None], (3, tok_count, dec_local, group_width))
    pre_recv, dec_recv = (
        lax.all_to_all(pre_send, "tok", split_axis=1, concat_axis=1, tiled=True),
        lax.all_to_all(dec_send, "tok", split_axis=1, concat_axis=1, tiled=True),
    )
    pre_recv = pre_recv.reshape(3, span_rows, group_width)
    dec_recv = dec_recv.reshape(3, dec_total, group_width)
    offset_now = pre_offsets[0]
    pre_att = prefill_attend(pre_recv, offset_now, pre_cache)
    pre_att, out_full, gate_up_full, down_full = lax.optimization_barrier(
        (pre_att, whole(w_out, 0), whole(w_gate_up, 2), whole(w_down, 0))
    )
    own_slots = lax.dynamic_slice_in_dim(dec_order, tok_index * dec_local, dec_local)
    dec_mine = jnp.take(dec_recv, own_slots, axis=1)
    dec_att = decode_attend(dec_mine, dec_lengths, dec_cache)
    picker = (jnp.arange(dec_total, dtype=jnp.int32)[:, None] == own_slots[None, :]).astype(
        jnp.bfloat16
    )
    dec_back = (
        jnp.dot(picker, dec_att, preferred_element_type=jnp.float32)
        .astype(jnp.bfloat16)
        .reshape(tok_count, dec_local, group_width)
    )
    pre_back = pre_att.reshape(tok_count, piece_len, group_width)
    pre_ret, dec_ret = (
        lax.all_to_all(pre_back, "tok", split_axis=0, concat_axis=0, tiled=True),
        lax.all_to_all(dec_back, "tok", split_axis=0, concat_axis=0, tiled=True),
    )
    slot_range = jnp.arange(tok_count, dtype=jnp.int32)
    inverse = jnp.sum(
        jnp.where(pre_order[None, :] == slot_range[:, None], slot_range[None, :], 0), axis=1
    )
    pre_mixed = jnp.take(pre_ret, inverse, axis=0).reshape(span_rows, group_width)
    dec_mixed = jnp.sum(dec_ret.astype(jnp.float32), axis=0).astype(jnp.bfloat16)
    attended = jnp.concatenate([pre_mixed, dec_mixed], axis=0)
    resid = rows.astype(jnp.float32) + over_heads(map_rows(attended, out_full))
    mlp_in = rms_norm(resid, mlp_gain)
    gate_up = fold_rows(mlp_in, gate_up_full)
    hidden = (jax.nn.silu(gate_up[0]) * gate_up[1]).astype(jnp.bfloat16)
    final = (resid + over_heads(map_rows(hidden, down_full))).astype(jnp.bfloat16)
    return (final[:span_rows], final[span_rows:])


def solution(mesh):
    placed = (
        P("tok", None),
        P("tok", None),
        P(),
        P(),
        P(None, "head", "tok"),
        P("tok", "head"),
        P(None, "head", "tok"),
        P("tok", "head"),
        P("tok", None, None, "head"),
        P("tok", None, None, "head"),
        P(),
        P(),
        P("tok"),
        P("tok"),
    )
    return jax.shard_map(
        on_device,
        mesh=mesh,
        in_specs=placed,
        out_specs=(P("tok", None), P("tok", None)),
        check_vma=False,
    )
```

```python
import jax
import jax.numpy as jnp
from jax import lax
from jax.experimental import pallas as pl
from jax.experimental.pallas import tpu as pltpu
from jax.sharding import PartitionSpec as P

HD = 64
Q_ROWS = 512
K_ROWS = 512
DEC_ROWS = 1024
DEC_PAD = 16


rope_base = 130000.0
norm_eps = 1e-05
masked_score = -1e30


def rotate(values, positions):
    width = values.shape[-1]
    half = width // 2
    freqs = rope_base ** (-(jnp.arange(half, dtype=jnp.float32) * 2.0 / width))
    angles = positions.astype(jnp.float32)[:, None] * freqs[None, :]
    cosine = jnp.cos(angles)[:, None, :]
    sine = jnp.sin(angles)[:, None, :]
    first = values[..., :half]
    second = values[..., half:]
    return jnp.concatenate(
        [first * cosine - second * sine, second * cosine + first * sine], axis=-1
    )


def rms_norm(rows, gain):
    rows = rows.astype(jnp.float32)
    factor = lax.rsqrt(jnp.mean(rows * rows, axis=-1, keepdims=True) + norm_eps)
    return (rows * factor * gain).astype(jnp.bfloat16)


def fold_rows(inputs, weights):
    return jnp.einsum("td,kcd->ktc", inputs, weights, preferred_element_type=jnp.float32)


def map_rows(inputs, weights):
    return jnp.einsum("tc,dc->td", inputs, weights, preferred_element_type=jnp.float32)


def whole(weights, axis):
    return lax.all_gather(weights, "tok", axis=axis, tiled=True)


def to_heads(blocks):
    return lax.all_to_all(blocks, "head", split_axis=0, concat_axis=0, tiled=True)


def from_heads(rows):
    return lax.all_gather(rows, "head", axis=0, tiled=True)


def sum_heads(partial_value):
    return lax.psum_scatter(
        partial_value.astype(jnp.bfloat16), "head", scatter_dimension=0, tiled=True
    )


def after(first, second):
    return lax.optimization_barrier((first, second))


def rope_tables(positions, width):
    half = HD // 2
    freqs = rope_base ** (-(jnp.arange(half, dtype=jnp.float32) * 2.0 / HD))
    angles = positions.astype(jnp.float32)[:, None] * freqs[None, :]
    cosine = jnp.cos(angles)
    sine = jnp.sin(angles)
    copies = width // HD
    return (
        jnp.tile(jnp.concatenate([cosine, cosine], axis=1), (1, copies)),
        jnp.tile(jnp.concatenate([-sine, sine], axis=1), (1, copies)),
    )


def swap_halves(values):
    half = HD // 2
    width = values.shape[-1]
    lane = lax.broadcasted_iota(jnp.int32, values.shape, values.ndim - 1)
    axis = values.ndim - 1
    return jnp.where(
        lane % HD < half,
        pltpu.roll(values, width - half, axis),
        pltpu.roll(values, half, axis),
    )


def prefill_kernel(
    limit_ref, q_ref, k_ref, v_ref, cos_ref, sin_ref, cache_ref, out_ref, q_rot, k_rot, v_ext, c_ext
):
    span = q_ref.shape[1]
    length = cache_ref.shape[2]
    pair = q_ref.shape[2]
    limit = limit_ref[0]
    cosine = cos_ref[...]
    sine = sin_ref[...]
    lane = lax.broadcasted_iota(jnp.int32, (1, pair), 1)
    halves = (lane < HD, lane >= HD)

    key = k_ref[0].astype(jnp.float32)
    k_rot[...] = (key * cosine + swap_halves(key) * sine).astype(jnp.bfloat16)
    query = q_ref[0].astype(jnp.float32)
    query = (query * cosine + swap_halves(query) * sine).astype(jnp.bfloat16)
    query = query * jnp.bfloat16(HD**-0.5)
    one = jnp.ones((), jnp.bfloat16)
    zero = jnp.zeros((), jnp.bfloat16)
    for side in range(2):
        q_rot[side] = jnp.where(halves[side], query, zero)
        v_ext[side] = jnp.where(halves[side], v_ref[0], one)
        c_ext[side] = jnp.where(halves[side], cache_ref[0, 1], one)

    def score(rows, keys):
        return lax.dot_general(
            rows, keys, (((1,), (1,)), ((), ())), preferred_element_type=jnp.float32
        )

    def fold(state, scores, values):
        top, mixed = state
        new_top = jnp.maximum(top, jnp.max(scores, axis=-1, keepdims=True))
        weights = jnp.exp(scores - new_top).astype(jnp.bfloat16)
        factor = jnp.exp(top - new_top)
        return new_top, mixed * factor + jnp.dot(
            weights, values, preferred_element_type=jnp.float32
        )

    for block in range(span // Q_ROWS):
        start = block * Q_ROWS
        rows = [q_rot[side, start : start + Q_ROWS, :] for side in range(2)]
        keys = k_rot[start : start + Q_ROWS, :]
        shape = (Q_ROWS, Q_ROWS)
        seen = lax.broadcasted_iota(jnp.int32, shape, 1) <= lax.broadcasted_iota(
            jnp.int32, shape, 0
        )
        states = []
        for side in range(2):
            scores = jnp.where(seen, score(rows[side], keys), masked_score)
            top = jnp.max(scores, axis=-1, keepdims=True)
            weights = jnp.exp(scores - top).astype(jnp.bfloat16)
            mixed = jnp.dot(
                weights,
                v_ext[side, start : start + Q_ROWS, :],
                preferred_element_type=jnp.float32,
            )
            states.append((top, mixed))
        for earlier in range(block):
            begin = earlier * Q_ROWS
            keys = k_rot[begin : begin + Q_ROWS, :]
            for side in range(2):
                states[side] = fold(
                    states[side],
                    score(rows[side], keys),
                    v_ext[side, begin : begin + Q_ROWS, :],
                )

        def cached(index, state, masked):
            begin = pl.multiple_of(index * K_ROWS, K_ROWS)
            keys_now = cache_ref[0, 0, pl.ds(begin, K_ROWS), :]
            result = []
            for side in range(2):
                scores = score(rows[side], keys_now)
                if masked:
                    spot = begin + lax.broadcasted_iota(jnp.int32, (1, K_ROWS), 1)
                    scores = jnp.where(spot < limit, scores, masked_score)
                result.append(
                    fold(state[side], scores, c_ext[side, pl.ds(begin, K_ROWS), :])
                )
            return tuple(result)

        full = limit // K_ROWS
        every = (limit + K_ROWS - 1) // K_ROWS
        states = lax.fori_loop(0, full, lambda i, s: cached(i, s, False), tuple(states))
        states = lax.fori_loop(full, every, lambda i, s: cached(i, s, True), states)
        parts = []
        for side in range(2):
            mixed = states[side][1]
            total = pltpu.roll(mixed, HD, 1)
            parts.append(mixed / total)
        out_ref[start : start + Q_ROWS, :] = jnp.where(halves[0], parts[0], parts[1]).astype(
            jnp.bfloat16
        )


def prefill_attend(qkv, offset, cache):
    _, span, width = qkv.shape
    length = cache.shape[2]
    pair = 2 * HD
    cosine, sine = rope_tables(offset + jnp.arange(span, dtype=jnp.int32), pair)
    part = lambda which: pl.BlockSpec((1, span, pair), lambda p, limit: (which, 0, p))
    table = pl.BlockSpec((span, pair), lambda p, limit: (0, 0))
    return pl.pallas_call(
        prefill_kernel,
        out_shape=jax.ShapeDtypeStruct((span, width), jnp.bfloat16),
        grid_spec=pltpu.PrefetchScalarGridSpec(
            num_scalar_prefetch=1,
            grid=(width // pair,),
            in_specs=[
                part(0),
                part(1),
                part(2),
                table,
                table,
                pl.BlockSpec((1, 2, length, pair), lambda p, limit: (0, 0, 0, p)),
            ],
            out_specs=pl.BlockSpec((span, pair), lambda p, limit: (0, p)),
            scratch_shapes=[
                pltpu.VMEM((2, span, pair), jnp.bfloat16),
                pltpu.VMEM((span, pair), jnp.bfloat16),
                pltpu.VMEM((2, span, pair), jnp.bfloat16),
                pltpu.VMEM((2, length, pair), jnp.bfloat16),
            ],
        ),
        compiler_params=pltpu.CompilerParams(vmem_limit_bytes=40 * 1024 * 1024),
        cost_estimate=pl.CostEstimate(
            flops=16 * span * 3 * span * width,
            bytes_accessed=4 * length * width + 8 * span * width,
            transcendentals=span * 3 * span * width // HD,
        ),
        name="prefill_attend",
    )(offset[None], qkv, qkv, qkv, cosine, sine, cache)


def decode_kernel(limits_ref, q_ref, k_ref, v_ref, cache_ref, out_ref, top_ref, total_ref, mixed_ref):
    request = pl.program_id(0)
    index = pl.program_id(1)
    limit = limits_ref[request]
    heads, width = q_ref.shape[1:]
    block = cache_ref.shape[2]

    @pl.when(index == 0)
    def _():
        own = q_ref[0].astype(jnp.float32) * k_ref[0].astype(jnp.float32)
        top_ref[...] = jnp.sum(own, axis=-1, keepdims=True)
        total_ref[...] = jnp.ones_like(total_ref)
        mixed_ref[...] = jnp.broadcast_to(v_ref[0].astype(jnp.float32), (heads, width))

    @pl.when(index * block < limit)
    def _():
        scores = lax.dot_general(
            q_ref[0],
            cache_ref[0, 0],
            (((1,), (1,)), ((), ())),
            preferred_element_type=jnp.float32,
        )
        spot = index * block + lax.broadcasted_iota(jnp.int32, (1, block), 1)
        scores = jnp.where(spot < limit, scores, masked_score)
        top = top_ref[...]
        new_top = jnp.maximum(top, jnp.max(scores, axis=-1, keepdims=True))
        weights = jnp.exp(scores - new_top)
        factor = jnp.exp(top - new_top)
        top_ref[...] = new_top
        total_ref[...] = total_ref[...] * factor + jnp.sum(weights, axis=-1, keepdims=True)
        mixed_ref[...] = mixed_ref[...] * factor + jnp.dot(
            weights.astype(jnp.bfloat16), cache_ref[0, 1], preferred_element_type=jnp.float32
        )

    @pl.when(index == pl.num_programs(1) - 1)
    def _():
        shape = (heads, width)
        mine = lax.broadcasted_iota(jnp.int32, shape, 1) // HD == lax.broadcasted_iota(
            jnp.int32, shape, 0
        )
        value = jnp.where(mine, mixed_ref[...] / total_ref[...], 0.0)
        out_ref[0] = jnp.sum(value, axis=0, keepdims=True).astype(jnp.bfloat16)


def decode_attend(qkv, lengths, cache):
    _, count, width = qkv.shape
    heads = width // HD
    block = min(DEC_ROWS, cache.shape[2])
    split = qkv.reshape(3, count, heads, HD)
    q_rot = rotate(split[0].astype(jnp.float32), lengths).astype(jnp.bfloat16)
    k_rot = rotate(split[1].astype(jnp.float32), lengths).astype(jnp.bfloat16)
    q_rot = q_rot * jnp.bfloat16(HD**-0.5)
    spread = jnp.where(
        jnp.eye(heads, dtype=jnp.bool_)[None, :, :, None], q_rot[:, None], jnp.bfloat16(0)
    ).reshape(count, heads, width)

    def cache_at(request, index, limits):
        last = (limits[request] - 1) // block
        return (request, 0, jnp.minimum(index, last), 0)

    row = pl.BlockSpec((1, 1, width), lambda request, index, limits: (request, 0, 0))
    return pl.pallas_call(
        decode_kernel,
        out_shape=jax.ShapeDtypeStruct((count, 1, width), jnp.bfloat16),
        grid_spec=pltpu.PrefetchScalarGridSpec(
            num_scalar_prefetch=1,
            grid=(count, cache.shape[2] // block),
            in_specs=[
                pl.BlockSpec((1, heads, width), lambda request, index, limits: (request, 0, 0)),
                row,
                row,
                pl.BlockSpec((1, 2, block, width), cache_at),
            ],
            out_specs=row,
            scratch_shapes=[
                pltpu.VMEM((heads, 1), jnp.float32),
                pltpu.VMEM((heads, 1), jnp.float32),
                pltpu.VMEM((heads, width), jnp.float32),
            ],
        ),
        compiler_params=pltpu.CompilerParams(vmem_limit_bytes=32 * 1024 * 1024),
        cost_estimate=pl.CostEstimate(
            flops=4 * count * heads * cache.shape[2] * width,
            bytes_accessed=4 * count * cache.shape[2] * width,
            transcendentals=count * cache.shape[2] * heads,
        ),
        name="decode_attend",
    )(lengths, spread, k_rot.reshape(count, 1, width), qkv[2].reshape(count, 1, width), cache)[:, 0]


def on_device(
    pre_tokens,
    dec_tokens,
    attn_gain,
    mlp_gain,
    w_qkv,
    w_out,
    w_gate_up,
    w_down,
    pre_cache,
    dec_cache,
    pre_order,
    dec_order,
    pre_offsets,
    dec_lengths,
):
    tok_count = lax.axis_size("tok")
    tok_index = lax.axis_index("tok")
    span_rows = pre_tokens.shape[0]
    piece_len = span_rows // tok_count
    dec_local = dec_tokens.shape[0]
    dec_total = dec_order.shape[0]
    group_width = w_qkv.shape[1]
    head_count = lax.axis_size("head")
    out_depth, out_width = w_out.shape
    out_rows = to_heads(jnp.broadcast_to(w_out[None], (head_count, out_depth, out_width)))
    out_rows = jnp.transpose(out_rows, (1, 0, 2)).reshape(out_depth, head_count * out_width)
    rows = jnp.concatenate([pre_tokens, dec_tokens], axis=0)
    normed = rms_norm(rows, attn_gain)
    projected = fold_rows(normed, whole(w_qkv, 2)).astype(jnp.bfloat16)
    pre_part = projected[:, :span_rows].reshape(3, tok_count, piece_len, group_width)
    pre_send = jnp.take(pre_part, pre_order, axis=1)
    dec_part = projected[:, span_rows:]
    dec_send = jnp.broadcast_to(dec_part[:, None], (3, tok_count, dec_local, group_width))
    pre_recv, dec_recv = (
        lax.all_to_all(pre_send, "tok", split_axis=1, concat_axis=1, tiled=True),
        lax.all_to_all(dec_send, "tok", split_axis=1, concat_axis=1, tiled=True),
    )
    pre_recv = pre_recv.reshape(3, span_rows, group_width)
    dec_recv = dec_recv.reshape(3, dec_total, group_width)
    offset_now = pre_offsets[0]
    pre_att = prefill_attend(pre_recv, offset_now, pre_cache)
    pre_att, out_full, gate_up_full, down_full = lax.optimization_barrier(
        (pre_att, whole(out_rows, 0), whole(w_gate_up, 2), whole(w_down, 0))
    )
    own_slots = lax.dynamic_slice_in_dim(dec_order, tok_index * dec_local, dec_local)
    dec_mine = jnp.take(dec_recv, own_slots, axis=1)
    dec_att = decode_attend(dec_mine, dec_lengths, dec_cache)
    picker = (jnp.arange(dec_total, dtype=jnp.int32)[:, None] == own_slots[None, :]).astype(
        jnp.bfloat16
    )
    dec_back = (
        jnp.dot(picker, dec_att, preferred_element_type=jnp.float32)
        .astype(jnp.bfloat16)
        .reshape(tok_count, dec_local, group_width)
    )
    pre_back = pre_att.reshape(tok_count, piece_len, group_width)
    pre_ret, dec_ret = (
        lax.all_to_all(pre_back, "tok", split_axis=0, concat_axis=0, tiled=True),
        lax.all_to_all(dec_back, "tok", split_axis=0, concat_axis=0, tiled=True),
    )
    slot_range = jnp.arange(tok_count, dtype=jnp.int32)
    inverse = jnp.sum(
        jnp.where(pre_order[None, :] == slot_range[:, None], slot_range[None, :], 0), axis=1
    )
    pre_mixed = jnp.take(pre_ret, inverse, axis=0).reshape(span_rows, group_width)
    dec_mixed = jnp.sum(dec_ret.astype(jnp.float32), axis=0).astype(jnp.bfloat16)
    share = span_rows // head_count
    half = share // 2
    dec_pad = ((0, DEC_PAD - dec_local), (0, 0))
    dec_blocks = jnp.broadcast_to(
        jnp.pad(dec_mixed, dec_pad)[None], (head_count, DEC_PAD, group_width)
    )
    mixed = to_heads(
        jnp.concatenate([pre_mixed.reshape(head_count, share, group_width), dec_blocks], axis=1)
    )
    attended = jnp.transpose(mixed, (1, 0, 2)).reshape(share + DEC_PAD, head_count * group_width)
    own_rows = jnp.concatenate(
        [
            lax.dynamic_slice_in_dim(pre_tokens, lax.axis_index("head") * share, share),
            jnp.pad(dec_tokens, dec_pad),
        ],
        axis=0,
    )
    resid = own_rows.astype(jnp.float32) + map_rows(attended, out_full)
    mlp_in = rms_norm(resid, mlp_gain)
    width = mlp_in.shape[1]

    def mlp_partial(inputs):
        gate_up = fold_rows(inputs, gate_up_full)
        hidden = (jax.nn.silu(gate_up[0]) * gate_up[1]).astype(jnp.bfloat16)
        return map_rows(hidden, down_full).astype(jnp.bfloat16)

    first_in = from_heads(mlp_in[:half])
    first_in, second_own = after(first_in, mlp_in[half:share])
    second_in = from_heads(second_own)
    first_part = mlp_partial(first_in)
    second_part = mlp_partial(jnp.concatenate([second_in, mlp_in[share:]], axis=0))
    wide = head_count * half
    second_part = jnp.concatenate(
        [
            second_part[:wide].reshape(head_count, half, width),
            jnp.broadcast_to(second_part[wide:][None], (head_count, DEC_PAD, width)),
        ],
        axis=1,
    ).reshape(head_count * (half + DEC_PAD), width)
    first_sum = sum_heads(first_part)
    first_sum, second_part = after(first_sum, second_part)
    second_sum = sum_heads(second_part)
    first_own = (resid[:half] + first_sum.astype(jnp.float32)).astype(jnp.bfloat16)
    first_own, second_sum = after(first_own, second_sum)
    first_out = from_heads(first_own)
    second_own = (resid[half:] + second_sum.astype(jnp.float32)).astype(jnp.bfloat16)
    first_out, second_own = after(first_out, second_own)
    second_out = from_heads(second_own).reshape(head_count, half + DEC_PAD, width)
    pre_out = jnp.concatenate(
        [first_out.reshape(head_count, half, width), second_out[:, :half]], axis=1
    ).reshape(span_rows, width)
    return (pre_out, second_out[0, half : half + dec_local])


def solution(mesh):
    placed = (
        P("tok", None),
        P("tok", None),
        P(),
        P(),
        P(None, "head", "tok"),
        P("tok", "head"),
        P(None, "head", "tok"),
        P("tok", "head"),
        P("tok", None, None, "head"),
        P("tok", None, None, "head"),
        P(),
        P(),
        P("tok"),
        P("tok"),
    )
    return jax.shard_map(
        on_device,
        mesh=mesh,
        in_specs=placed,
        out_specs=(P("tok", None), P("tok", None)),
        check_vma=False,
    )
```

```python
import jax
import jax.numpy as jnp
from jax import lax
from jax.experimental import pallas as pl
from jax.experimental.pallas import tpu as pltpu
from jax.sharding import PartitionSpec as P

HD = 64
Q_ROWS = 512
K_ROWS = 512
DEC_ROWS = 1024
DEC_PAD = 16


rope_base = 130000.0
norm_eps = 1e-05
masked_score = -1e30


def rotate(values, positions):
    width = values.shape[-1]
    half = width // 2
    freqs = rope_base ** (-(jnp.arange(half, dtype=jnp.float32) * 2.0 / width))
    angles = positions.astype(jnp.float32)[:, None] * freqs[None, :]
    cosine = jnp.cos(angles)[:, None, :]
    sine = jnp.sin(angles)[:, None, :]
    first = values[..., :half]
    second = values[..., half:]
    return jnp.concatenate(
        [first * cosine - second * sine, second * cosine + first * sine], axis=-1
    )


def rms_norm(rows, gain):
    rows = rows.astype(jnp.float32)
    factor = lax.rsqrt(jnp.mean(rows * rows, axis=-1, keepdims=True) + norm_eps)
    return (rows * factor * gain).astype(jnp.bfloat16)


def fold_rows(inputs, weights):
    return jnp.einsum("td,kcd->ktc", inputs, weights, preferred_element_type=jnp.float32)


def map_rows(inputs, weights):
    return jnp.einsum("tc,dc->td", inputs, weights, preferred_element_type=jnp.float32)


def whole(weights, axis):
    return lax.all_gather(weights, "tok", axis=axis, tiled=True)


def to_heads(blocks):
    return lax.all_to_all(blocks, "head", split_axis=0, concat_axis=0, tiled=True)


def from_heads(rows):
    return lax.all_gather(rows, "head", axis=0, tiled=True)


def sum_heads(partial_value):
    return lax.psum_scatter(
        partial_value.astype(jnp.bfloat16), "head", scatter_dimension=0, tiled=True
    )


def after(first, second):
    return lax.optimization_barrier((first, second))


def rope_tables(positions, width):
    half = HD // 2
    freqs = rope_base ** (-(jnp.arange(half, dtype=jnp.float32) * 2.0 / HD))
    angles = positions.astype(jnp.float32)[:, None] * freqs[None, :]
    cosine = jnp.cos(angles)
    sine = jnp.sin(angles)
    copies = width // HD
    return (
        jnp.tile(jnp.concatenate([cosine, cosine], axis=1), (1, copies)),
        jnp.tile(jnp.concatenate([-sine, sine], axis=1), (1, copies)),
    )


def swap_halves(values):
    half = HD // 2
    width = values.shape[-1]
    lane = lax.broadcasted_iota(jnp.int32, values.shape, values.ndim - 1)
    axis = values.ndim - 1
    return jnp.where(
        lane % HD < half,
        pltpu.roll(values, width - half, axis),
        pltpu.roll(values, half, axis),
    )


def prefill_kernel(
    limit_ref, q_ref, k_ref, v_ref, cos_ref, sin_ref, cache_ref, out_ref, q_rot, k_rot, v_ext, c_ext
):
    span = q_ref.shape[1]
    length = cache_ref.shape[2]
    pair = q_ref.shape[2]
    limit = limit_ref[0]
    cosine = cos_ref[...]
    sine = sin_ref[...]
    lane = lax.broadcasted_iota(jnp.int32, (1, pair), 1)
    halves = (lane < HD, lane >= HD)

    key = k_ref[0].astype(jnp.float32)
    k_rot[...] = (key * cosine + swap_halves(key) * sine).astype(jnp.bfloat16)
    query = q_ref[0].astype(jnp.float32)
    query = (query * cosine + swap_halves(query) * sine).astype(jnp.bfloat16)
    query = query * jnp.bfloat16(HD**-0.5)
    one = jnp.ones((), jnp.bfloat16)
    zero = jnp.zeros((), jnp.bfloat16)
    for side in range(2):
        q_rot[side] = jnp.where(halves[side], query, zero)
        v_ext[side] = jnp.where(halves[side], v_ref[0], one)
        c_ext[side] = jnp.where(halves[side], cache_ref[0, 1], one)

    def score(rows, keys):
        return lax.dot_general(
            rows, keys, (((1,), (1,)), ((), ())), preferred_element_type=jnp.float32
        )

    def fold(state, scores, values):
        top, mixed = state
        new_top = jnp.maximum(top, jnp.max(scores, axis=-1, keepdims=True))
        weights = jnp.exp(scores - new_top).astype(jnp.bfloat16)
        factor = jnp.exp(top - new_top)
        return new_top, mixed * factor + jnp.dot(
            weights, values, preferred_element_type=jnp.float32
        )

    for block in range(span // Q_ROWS):
        start = block * Q_ROWS
        rows = [q_rot[side, start : start + Q_ROWS, :] for side in range(2)]
        keys = k_rot[start : start + Q_ROWS, :]
        shape = (Q_ROWS, Q_ROWS)
        seen = lax.broadcasted_iota(jnp.int32, shape, 1) <= lax.broadcasted_iota(
            jnp.int32, shape, 0
        )
        states = []
        for side in range(2):
            scores = jnp.where(seen, score(rows[side], keys), masked_score)
            top = jnp.max(scores, axis=-1, keepdims=True)
            weights = jnp.exp(scores - top).astype(jnp.bfloat16)
            mixed = jnp.dot(
                weights,
                v_ext[side, start : start + Q_ROWS, :],
                preferred_element_type=jnp.float32,
            )
            states.append((top, mixed))
        for earlier in range(block):
            begin = earlier * Q_ROWS
            keys = k_rot[begin : begin + Q_ROWS, :]
            for side in range(2):
                states[side] = fold(
                    states[side],
                    score(rows[side], keys),
                    v_ext[side, begin : begin + Q_ROWS, :],
                )

        def cached(index, state, masked):
            begin = pl.multiple_of(index * K_ROWS, K_ROWS)
            keys_now = cache_ref[0, 0, pl.ds(begin, K_ROWS), :]
            result = []
            for side in range(2):
                scores = score(rows[side], keys_now)
                if masked:
                    spot = begin + lax.broadcasted_iota(jnp.int32, (1, K_ROWS), 1)
                    scores = jnp.where(spot < limit, scores, masked_score)
                result.append(
                    fold(state[side], scores, c_ext[side, pl.ds(begin, K_ROWS), :])
                )
            return tuple(result)

        full = limit // K_ROWS
        every = (limit + K_ROWS - 1) // K_ROWS
        states = lax.fori_loop(0, full, lambda i, s: cached(i, s, False), tuple(states))
        states = lax.fori_loop(full, every, lambda i, s: cached(i, s, True), states)
        parts = []
        for side in range(2):
            mixed = states[side][1]
            total = pltpu.roll(mixed, HD, 1)
            parts.append(mixed / total)
        out_ref[start : start + Q_ROWS, :] = jnp.where(halves[0], parts[0], parts[1]).astype(
            jnp.bfloat16
        )


def prefill_attend(qkv, offset, cache):
    _, span, width = qkv.shape
    length = cache.shape[2]
    pair = 2 * HD
    cosine, sine = rope_tables(offset + jnp.arange(span, dtype=jnp.int32), pair)
    part = lambda which: pl.BlockSpec((1, span, pair), lambda p, limit: (which, 0, p))
    table = pl.BlockSpec((span, pair), lambda p, limit: (0, 0))
    return pl.pallas_call(
        prefill_kernel,
        out_shape=jax.ShapeDtypeStruct((span, width), jnp.bfloat16),
        grid_spec=pltpu.PrefetchScalarGridSpec(
            num_scalar_prefetch=1,
            grid=(width // pair,),
            in_specs=[
                part(0),
                part(1),
                part(2),
                table,
                table,
                pl.BlockSpec((1, 2, length, pair), lambda p, limit: (0, 0, 0, p)),
            ],
            out_specs=pl.BlockSpec((span, pair), lambda p, limit: (0, p)),
            scratch_shapes=[
                pltpu.VMEM((2, span, pair), jnp.bfloat16),
                pltpu.VMEM((span, pair), jnp.bfloat16),
                pltpu.VMEM((2, span, pair), jnp.bfloat16),
                pltpu.VMEM((2, length, pair), jnp.bfloat16),
            ],
        ),
        compiler_params=pltpu.CompilerParams(vmem_limit_bytes=40 * 1024 * 1024),
        cost_estimate=pl.CostEstimate(
            flops=16 * span * 3 * span * width,
            bytes_accessed=4 * length * width + 8 * span * width,
            transcendentals=span * 3 * span * width // HD,
        ),
        name="prefill_attend",
    )(offset[None], qkv, qkv, qkv, cosine, sine, cache)


def decode_kernel(limits_ref, q_ref, k_ref, v_ref, cache_ref, out_ref, top_ref, total_ref, mixed_ref):
    request = pl.program_id(0)
    index = pl.program_id(1)
    limit = limits_ref[request]
    heads, width = q_ref.shape[1:]
    block = cache_ref.shape[2]

    @pl.when(index == 0)
    def _():
        own = q_ref[0].astype(jnp.float32) * k_ref[0].astype(jnp.float32)
        top_ref[...] = jnp.sum(own, axis=-1, keepdims=True)
        total_ref[...] = jnp.ones_like(total_ref)
        mixed_ref[...] = jnp.broadcast_to(v_ref[0].astype(jnp.float32), (heads, width))

    @pl.when(index * block < limit)
    def _():
        scores = lax.dot_general(
            q_ref[0],
            cache_ref[0, 0],
            (((1,), (1,)), ((), ())),
            preferred_element_type=jnp.float32,
        )
        spot = index * block + lax.broadcasted_iota(jnp.int32, (1, block), 1)
        scores = jnp.where(spot < limit, scores, masked_score)
        top = top_ref[...]
        new_top = jnp.maximum(top, jnp.max(scores, axis=-1, keepdims=True))
        weights = jnp.exp(scores - new_top)
        factor = jnp.exp(top - new_top)
        top_ref[...] = new_top
        total_ref[...] = total_ref[...] * factor + jnp.sum(weights, axis=-1, keepdims=True)
        mixed_ref[...] = mixed_ref[...] * factor + jnp.dot(
            weights.astype(jnp.bfloat16), cache_ref[0, 1], preferred_element_type=jnp.float32
        )

    @pl.when(index == pl.num_programs(1) - 1)
    def _():
        shape = (heads, width)
        mine = lax.broadcasted_iota(jnp.int32, shape, 1) // HD == lax.broadcasted_iota(
            jnp.int32, shape, 0
        )
        value = jnp.where(mine, mixed_ref[...] / total_ref[...], 0.0)
        out_ref[0] = jnp.sum(value, axis=0, keepdims=True).astype(jnp.bfloat16)


def decode_attend(qkv, lengths, cache):
    _, count, width = qkv.shape
    heads = width // HD
    block = min(DEC_ROWS, cache.shape[2])
    split = qkv.reshape(3, count, heads, HD)
    q_rot = rotate(split[0].astype(jnp.float32), lengths).astype(jnp.bfloat16)
    k_rot = rotate(split[1].astype(jnp.float32), lengths).astype(jnp.bfloat16)
    q_rot = q_rot * jnp.bfloat16(HD**-0.5)
    spread = jnp.where(
        jnp.eye(heads, dtype=jnp.bool_)[None, :, :, None], q_rot[:, None], jnp.bfloat16(0)
    ).reshape(count, heads, width)

    def cache_at(request, index, limits):
        last = (limits[request] - 1) // block
        return (request, 0, jnp.minimum(index, last), 0)

    row = pl.BlockSpec((1, 1, width), lambda request, index, limits: (request, 0, 0))
    return pl.pallas_call(
        decode_kernel,
        out_shape=jax.ShapeDtypeStruct((count, 1, width), jnp.bfloat16),
        grid_spec=pltpu.PrefetchScalarGridSpec(
            num_scalar_prefetch=1,
            grid=(count, cache.shape[2] // block),
            in_specs=[
                pl.BlockSpec((1, heads, width), lambda request, index, limits: (request, 0, 0)),
                row,
                row,
                pl.BlockSpec((1, 2, block, width), cache_at),
            ],
            out_specs=row,
            scratch_shapes=[
                pltpu.VMEM((heads, 1), jnp.float32),
                pltpu.VMEM((heads, 1), jnp.float32),
                pltpu.VMEM((heads, width), jnp.float32),
            ],
        ),
        compiler_params=pltpu.CompilerParams(vmem_limit_bytes=32 * 1024 * 1024),
        cost_estimate=pl.CostEstimate(
            flops=4 * count * heads * cache.shape[2] * width,
            bytes_accessed=4 * count * cache.shape[2] * width,
            transcendentals=count * cache.shape[2] * heads,
        ),
        name="decode_attend",
    )(lengths, spread, k_rot.reshape(count, 1, width), qkv[2].reshape(count, 1, width), cache)[:, 0]


def on_device(
    pre_tokens,
    dec_tokens,
    attn_gain,
    mlp_gain,
    w_qkv,
    w_out,
    w_gate_up,
    w_down,
    pre_cache,
    dec_cache,
    pre_order,
    dec_order,
    pre_offsets,
    dec_lengths,
):
    tok_count = lax.axis_size("tok")
    tok_index = lax.axis_index("tok")
    span_rows = pre_tokens.shape[0]
    piece_len = span_rows // tok_count
    dec_local = dec_tokens.shape[0]
    dec_total = dec_order.shape[0]
    group_width = w_qkv.shape[1]
    head_count = lax.axis_size("head")
    out_depth, out_width = w_out.shape
    out_rows = to_heads(jnp.broadcast_to(w_out[None], (head_count, out_depth, out_width)))
    out_rows = jnp.transpose(out_rows, (1, 0, 2)).reshape(out_depth, head_count * out_width)
    rows = jnp.concatenate([pre_tokens, dec_tokens], axis=0)
    normed = rms_norm(rows, attn_gain)
    projected = fold_rows(normed, whole(w_qkv, 2)).astype(jnp.bfloat16)
    pre_part = projected[:, :span_rows].reshape(3, tok_count, piece_len, group_width)
    pre_send = jnp.take(pre_part, pre_order, axis=1)
    dec_part = projected[:, span_rows:]
    dec_send = jnp.broadcast_to(dec_part[:, None], (3, tok_count, dec_local, group_width))
    pre_recv, dec_recv = (
        lax.all_to_all(pre_send, "tok", split_axis=1, concat_axis=1, tiled=True),
        lax.all_to_all(dec_send, "tok", split_axis=1, concat_axis=1, tiled=True),
    )
    pre_recv = pre_recv.reshape(3, span_rows, group_width)
    dec_recv = dec_recv.reshape(3, dec_total, group_width)
    offset_now = pre_offsets[0]
    pre_att = prefill_attend(pre_recv, offset_now, pre_cache)
    out_full = whole(out_rows, 0)
    own_slots = lax.dynamic_slice_in_dim(dec_order, tok_index * dec_local, dec_local)
    dec_mine = jnp.take(dec_recv, own_slots, axis=1)
    dec_att = decode_attend(dec_mine, dec_lengths, dec_cache)
    picker = (jnp.arange(dec_total, dtype=jnp.int32)[:, None] == own_slots[None, :]).astype(
        jnp.bfloat16
    )
    dec_back = (
        jnp.dot(picker, dec_att, preferred_element_type=jnp.float32)
        .astype(jnp.bfloat16)
        .reshape(tok_count, dec_local, group_width)
    )
    pre_back = pre_att.reshape(tok_count, piece_len, group_width)
    pre_ret, dec_ret = (
        lax.all_to_all(pre_back, "tok", split_axis=0, concat_axis=0, tiled=True),
        lax.all_to_all(dec_back, "tok", split_axis=0, concat_axis=0, tiled=True),
    )
    slot_range = jnp.arange(tok_count, dtype=jnp.int32)
    inverse = jnp.sum(
        jnp.where(pre_order[None, :] == slot_range[:, None], slot_range[None, :], 0), axis=1
    )
    pre_mixed = jnp.take(pre_ret, inverse, axis=0).reshape(span_rows, group_width)
    dec_mixed = jnp.sum(dec_ret.astype(jnp.float32), axis=0).astype(jnp.bfloat16)
    share = span_rows // head_count
    half = share // 2
    dec_pad = ((0, DEC_PAD - dec_local), (0, 0))
    dec_blocks = jnp.broadcast_to(
        jnp.pad(dec_mixed, dec_pad)[None], (head_count, DEC_PAD, group_width)
    )
    mixed = to_heads(
        jnp.concatenate([pre_mixed.reshape(head_count, share, group_width), dec_blocks], axis=1)
    )
    attended = jnp.transpose(mixed, (1, 0, 2)).reshape(share + DEC_PAD, head_count * group_width)
    own_rows = jnp.concatenate(
        [
            lax.dynamic_slice_in_dim(pre_tokens, lax.axis_index("head") * share, share),
            jnp.pad(dec_tokens, dec_pad),
        ],
        axis=0,
    )
    resid = own_rows.astype(jnp.float32) + map_rows(attended, out_full)
    mlp_in = rms_norm(resid, mlp_gain)
    width = mlp_in.shape[1]
    mlp_in, gate_up_full, down_full = lax.optimization_barrier(
        (mlp_in, whole(w_gate_up, 2), whole(w_down, 0))
    )

    def mlp_partial(inputs):
        gate_up = fold_rows(inputs, gate_up_full)
        hidden = (jax.nn.silu(gate_up[0]) * gate_up[1]).astype(jnp.bfloat16)
        return map_rows(hidden, down_full).astype(jnp.bfloat16)

    first_in = from_heads(mlp_in[:half])
    first_in, second_own = after(first_in, mlp_in[half:share])
    second_in = from_heads(second_own)
    first_part = mlp_partial(first_in)
    second_part = mlp_partial(jnp.concatenate([second_in, mlp_in[share:]], axis=0))
    wide = head_count * half
    second_part = jnp.concatenate(
        [
            second_part[:wide].reshape(head_count, half, width),
            jnp.broadcast_to(second_part[wide:][None], (head_count, DEC_PAD, width)),
        ],
        axis=1,
    ).reshape(head_count * (half + DEC_PAD), width)
    first_sum = sum_heads(first_part)
    first_sum, second_part = after(first_sum, second_part)
    second_sum = sum_heads(second_part)
    first_own = (resid[:half] + first_sum.astype(jnp.float32)).astype(jnp.bfloat16)
    first_own, second_sum = after(first_own, second_sum)
    first_out = from_heads(first_own)
    second_own = (resid[half:] + second_sum.astype(jnp.float32)).astype(jnp.bfloat16)
    first_out, second_own = after(first_out, second_own)
    second_out = from_heads(second_own).reshape(head_count, half + DEC_PAD, width)
    pre_out = jnp.concatenate(
        [first_out.reshape(head_count, half, width), second_out[:, :half]], axis=1
    ).reshape(span_rows, width)
    return (pre_out, second_out[0, half : half + dec_local])


def solution(mesh):
    placed = (
        P("tok", None),
        P("tok", None),
        P(),
        P(),
        P(None, "head", "tok"),
        P("tok", "head"),
        P(None, "head", "tok"),
        P("tok", "head"),
        P("tok", None, None, "head"),
        P("tok", None, None, "head"),
        P(),
        P(),
        P("tok"),
        P("tok"),
    )
    return jax.shard_map(
        on_device,
        mesh=mesh,
        in_specs=placed,
        out_specs=(P("tok", None), P("tok", None)),
        check_vma=False,
    )
```
